32 devices in a mesh: dp: 4 (over z), expert: 8 (over y, x, core).
Axes of the slice: x: 2, y: 2, z: 4, core: 2. Of those that a mesh axis runs over, the one named last changes fastest.
Arguments:
- attn_out: bfloat16 [2048, 4096], P('dp', 'expert'), may hold values from -6 to 6
- out_weight: bfloat16 [4096, 2880], P('expert'), may hold values from -0.09375 to 0.09375
- out_bias: float32 [2880], replicated, may hold values from -3 to 3
- residual_in: bfloat16 [2048, 2880], P(('dp', 'expert')), may hold values from -6 to 6
- norm_gain: float32 [2880], replicated, may hold values from 0.25 to 1.75
- router_weight: bfloat16 [2880, 8], replicated, may hold values from -0.109375 to 0.109375
- router_bias: float32 [8], replicated, may hold values from -1 to 332
- expert_ids: int32 [2048, 4], P(('dp', 'expert')), may hold values from 0 to 7, all different within a row; in each aligned block of 64 rows (0 to 63, 64 to 127, ...) at most 64 rows name the same one
- filled_rows: int32 [32], P(('dp', 'expert')), may hold values from 1 to 64, as said below
- gate_up: bfloat16 [8, 2, 1440, 2880], P('expert', None, 'dp'), may hold values from -0.33398438 to 0.33398438
- gate_up_bias: float32 [8, 2, 1440], P('expert'), may hold values from -3 to 3
- down_weight: bfloat16 [8, 1440, 2880], P('expert', 'dp'), may hold values from -0.04736328 to 0.04736328
- down_bias: float32 [8, 2880], P('expert'), may hold values from -2 to 2
- next_gain: float32 [2880], replicated, may hold values from 0.25 to 1.75
Outputs:
- stream: bfloat16 [2048, 2880], P(('dp', 'expert'))
- normed_next: bfloat16 [2048, 2880], P(('dp', 'expert'))
The draws below stay inside these ranges and needn't reach their ends.
Inputs may be any that keep to these rules, and one draw needn't show every extreme that they name: `expert_ids`: within each device's 64 rows (aligned blocks) no expert is named by more than 64 rows, a bound that some block reaches. `filled_rows`: some block is full.
All inputs are finite; a program needn't handle non-finite values.
Results may differ from the reference program's by a relative error of at most 0.015.
Values may be sent and summed in bfloat16 or wider, within the bound.
A program may use at most 192 MiB of HBM per device.

```python
import math
import jax
import jax.numpy as jnp
import numpy as np
from jax import lax

D = 2880
ATTN = 4096
TOP = 4
FFW = 1440
TOK_DEV = 64
EXPERTS = 8
CAP = 64
BLOCKS = 32
TOKENS = 2048
N_EXPERT = 8


def draw_router_bias(key, part):
    base = jax.random.uniform(key, (EXPERTS,), jnp.float32, -1.0, 1.0)
    return base


def draw_filled_rows(key, part):
    counts = jax.random.randint(jax.random.fold_in(key, 3), (BLOCKS,), 1, TOK_DEV + 1)
    spot = jax.random.randint(jax.random.fold_in(key, 5), (), 0, BLOCKS)
    return counts.at[spot].set(TOK_DEV).astype(jnp.int32)


def strengthened(values, key, source, target, shards_of, factor):
    owner, partner = [(jnp.arange(values.shape[position]) // (values.shape[position] // shards_of)).reshape([-1 if axis == position else 1 for axis in range(values.ndim)]) for position in (source, target)]
    chosen = jax.random.permutation(key, shards_of)[partner]
    strong = (owner == chosen) | (owner == (partner + shards_of // 2) % shards_of)
    return jnp.where(strong, factor * values, values)


def shard_levels(stream_key, dims, shards, low, top_value):
    level = 1.0
    for dim, blocks in shards:
        draws = jax.random.uniform(jax.random.fold_in(jax.random.fold_in(stream_key, 6), dim), (blocks,), jnp.float32, low / len(shards), top_value / len(shards))
        level = level * jnp.repeat(jnp.exp(draws), dims[dim] // blocks).reshape((-1,) + (1,) * (len(dims) - 1 - dim))
    return level


def shared_out(rng, own, number, rows, count, top, bound, lean):
    ranking = jax.random.permutation(rng, count)
    heavy_load, common = shares(count, rows * top, bound, lean, True), shares(count, rows * top, bound, lean, False)
    places = jnp.arange(count)

    def named(tallies, offset_by):
        used = int((tallies > 0).sum())
        fixed = max(1, used // 4)
        shifted = fixed + (places - fixed + offset_by * (used - fixed)) % max(1, count - fixed)
        return jnp.zeros((count,), jnp.int32).at[ranking[jnp.where(places < fixed, places, shifted)]].set(jnp.asarray(tallies, jnp.int32))

    tallies = jnp.where(number % 4 == 0, named(heavy_load, number // 4), named(common, number - number // 4 - 1))
    mixed = jax.random.permutation(jax.random.fold_in(own, 3), count)
    giver, receiver = mixed[0:count // 2 * 2:2], mixed[1:count // 2 * 2:2]
    margin = jnp.minimum(tallies[giver] - 1, bound - tallies[receiver]) // 2
    margin = jnp.where((giver == ranking[0]) | (receiver == ranking[0]) | (tallies[receiver] == 0), 0, jnp.maximum(margin, 0))
    shifted = jax.random.randint(jax.random.fold_in(own, 4), (count // 2,), 0, 1 << 20) % (margin + 1)
    tallies = tallies.at[giver].add(-shifted).at[receiver].add(shifted)
    items = jnp.searchsorted(jnp.cumsum(tallies), jnp.arange(rows * top), side="right").astype(jnp.int32)
    grid = items.reshape(top, rows).T
    grid = grid[jax.random.permutation(jax.random.fold_in(own, 1), rows)]
    offset_by = jax.random.randint(jax.random.fold_in(own, 2), (rows, 1), 0, top)
    return jnp.take_along_axis(grid, (jnp.arange(top)[None, :] + offset_by) % top, axis=1)


def shares(number_of, total, most, lean, full):
    loads = [(1 << 20) // math.isqrt(rank ** lean) + 1 for rank in range(1, number_of + 1)]
    largest = most if full else min(most, max(-(-total // number_of), total * loads[0] // sum(loads)))
    least = 1 if total - largest >= number_of - 1 else 0
    given, rest = [largest] + [least] * (number_of - 1), total - largest - least * (number_of - 1)
    while rest > 0:
        movable = [i for i in range(1, number_of) if given[i] < largest] or [i for i in range(1, number_of) if given[i] < most]
        pool, budget = sum([loads[i] for i in movable]), rest
        for i in movable:
            more = min(most - given[i], max(1, budget * loads[i] // pool), rest)
            given[i] = given[i] + more
            rest = rest - more
    return np.array(given)


def centred(rng, extent, deviation, bound, shards=(), kind=jnp.bfloat16):
    values = deviation * jax.random.normal(rng, extent, jnp.float32)
    if shards:
        values = values * shard_levels(rng, extent, shards, -0.22, 0.18)
    return jnp.clip(values, -bound, bound).astype(kind)


def heavy_noise(rng, dims, width, limit, cuts, heavy, held_as=jnp.bfloat16):
    entries = width * jax.random.normal(rng, dims, jnp.float32)
    if cuts:
        entries = entries * shard_levels(rng, dims, cuts, -0.22, 0.18)
    return jnp.clip(strengthened(entries, jax.random.fold_in(rng, 3), *heavy), -limit, limit).astype(held_as)


def setup_inputs(seed: int = 0) -> dict:
    splits = jax.random.split(jax.random.key(seed), 15)
    attn_out = heavy_noise(splits[0], (TOKENS, ATTN), 1.0, 6.0, ((0, 4), (1, 8)), (1, 0, 8, 2.0))
    out_weight = centred(splits[1], (ATTN, D), ATTN ** -0.5, 0.09375, ((0, 8),))
    out_bias = centred(splits[2], (D,), 0.5, 3.0, (), jnp.float32)
    residual_in = centred(splits[3], (TOKENS, D), 1.0, 6.0, ((0, 32),))
    norm_gain = jnp.clip(1.0 + 0.15 * jax.random.normal(splits[4], (D,), jnp.float32), 0.25, 1.75)
    router_weight = centred(splits[5], (D, EXPERTS), D ** -0.5, 0.109375)
    router_bias = draw_router_bias(jax.random.fold_in(splits[14], 71), 0)
    expert_ids_keys = jax.random.split(jax.random.fold_in(splits[7], 1), TOKENS // TOK_DEV)
    expert_ids_turns = jax.random.permutation(jax.random.fold_in(splits[7], 3), TOKENS // TOK_DEV)
    expert_ids = jax.vmap(lambda own, number: shared_out(jax.random.fold_in(splits[7], 2), own, number, TOK_DEV, EXPERTS, TOP, CAP, 2))(expert_ids_keys, expert_ids_turns).reshape((TOKENS, TOP))
    filled_rows = draw_filled_rows(jax.random.fold_in(splits[14], 71), 0)
    gate_up = centred(splits[9], (EXPERTS, 2, FFW, D), (3.0 * D ** -0.5), 0.33398438, ((0, 8), (2, 4)))
    gate_up_bias = centred(splits[10], (EXPERTS, 2, FFW), 0.5, 3.0, ((0, 8),), jnp.float32)
    down_weight = centred(splits[11], (EXPERTS, FFW, D), (0.3 * FFW ** -0.5), 0.04736328, ((0, 8), (1, 4)))
    down_bias = centred(splits[12], (EXPERTS, D), 0.3, 2.0, ((0, 8),), jnp.float32)
    next_gain = jnp.clip(1.0 + 0.15 * jax.random.normal(splits[13], (D,), jnp.float32), 0.25, 1.75)
    return dict(attn_out=attn_out, out_weight=out_weight, out_bias=out_bias, residual_in=residual_in, norm_gain=norm_gain, router_weight=router_weight, router_bias=router_bias, expert_ids=expert_ids, filled_rows=filled_rows, gate_up=gate_up, gate_up_bias=gate_up_bias, down_weight=down_weight, down_bias=down_bias, next_gain=next_gain)


EPS = 1e-05
LIMIT = 7.0
ALPHA = 1.702

def normalize(values, gain):
    return values * lax.rsqrt(lax.optimization_barrier(jnp.mean(values * values, axis=-1, keepdims=True)) + EPS) * gain

def activate(gate_part, up_part):
    gate_part = jnp.minimum(gate_part, LIMIT)
    up_part = jnp.clip(up_part, -LIMIT, LIMIT)
    return ((up_part + 1.0) * gate_part * jax.nn.sigmoid(ALPHA * gate_part)).astype(jnp.bfloat16)

def reference(attn_out, out_weight, out_bias, residual_in, norm_gain, router_weight, router_bias, expert_ids, filled_rows, gate_up, gate_up_bias, down_weight, down_bias, next_gain):
    head_width = ATTN // N_EXPERT
    attn_parts = attn_out.reshape(TOKENS, N_EXPERT, head_width).transpose(1, 0, 2)
    weight_parts = out_weight.reshape(N_EXPERT, head_width, D)

    def add_part(running, pair_in):
        partial_sum = jnp.dot(pair_in[0], pair_in[1], preferred_element_type=jnp.float32)
        rounded = lax.optimization_barrier(partial_sum.astype(jnp.bfloat16))
        return (running + rounded.astype(jnp.float32), None)
    summed, unused = lax.scan(add_part, jnp.zeros((TOKENS, D), jnp.float32), (attn_parts, weight_parts))
    hidden_state = residual_in.astype(jnp.float32) + summed + out_bias
    normed_in = normalize(hidden_state, norm_gain).astype(jnp.bfloat16)
    logits = jnp.dot(normed_in, router_weight, preferred_element_type=jnp.float32) + router_bias
    chosen = jnp.take_along_axis(logits, expert_ids, axis=1)
    route_probs = jax.nn.softmax(chosen, axis=-1)
    positions = jnp.arange(TOKENS, dtype=jnp.int32)
    live_rows = positions % TOK_DEV < filled_rows[positions // TOK_DEV]
    route_weights = route_probs * live_rows[:, None].astype(jnp.float32)
    flat_ids = expert_ids.reshape(-1)
    flat_weights = route_weights.reshape(-1)
    most_rows = BLOCKS * CAP

    def one_expert(running, expert_index):
        hit_mask = flat_ids == expert_index
        found_rows = jnp.nonzero(hit_mask, size=most_rows, fill_value=0)[0].astype(jnp.int32)
        valid_rows = jnp.arange(most_rows, dtype=jnp.int32) < jnp.sum(hit_mask.astype(jnp.int32))
        token_index = found_rows // TOP
        row_block = normed_in[token_index].astype(jnp.float32)
        pair_weights = gate_up[expert_index].astype(jnp.float32)
        gate_part = jnp.dot(row_block, pair_weights[0].T) + gate_up_bias[expert_index, 0]
        up_part = jnp.dot(row_block, pair_weights[1].T) + gate_up_bias[expert_index, 1]
        hidden = activate(gate_part, up_part)
        result = jnp.dot(hidden.astype(jnp.float32), down_weight[expert_index].astype(jnp.float32)) + down_bias[expert_index]
        result = result.astype(jnp.bfloat16)
        contrib = result.astype(jnp.float32) * flat_weights[found_rows][:, None]
        target = jnp.where(valid_rows, token_index, TOKENS)
        return (running.at[target].add(contrib, mode='drop'), None)
    mixture, unused = lax.scan(one_expert, jnp.zeros((TOKENS, D), jnp.float32), jnp.arange(EXPERTS, dtype=jnp.int32))
    stream_full = hidden_state + mixture
    return (stream_full.astype(jnp.bfloat16), normalize(stream_full, next_gain).astype(jnp.bfloat16))
```

```python
import jax
import jax.numpy as jnp
from jax import lax
from jax.sharding import PartitionSpec as P

EPS = 1e-05
LIMIT = 7.0
ALPHA = 1.702


def normalize(values, gain):
    return values * lax.rsqrt(jnp.mean(values * values, axis=-1, keepdims=True) + EPS) * gain


def activate(gate_part, up_part):
    gate_part = jnp.minimum(gate_part, LIMIT)
    up_part = jnp.clip(up_part, -LIMIT, LIMIT)
    return ((up_part + 1.0) * gate_part * jax.nn.sigmoid(ALPHA * gate_part)).astype(jnp.bfloat16)


def hidden_units(row_block, pair_weights, bias_part):
    numbers = (((1,), (1,)), ((), ()))
    gate_part = (
        lax.dot_general(row_block, pair_weights[0], numbers, preferred_element_type=jnp.float32)
        + bias_part[0]
    )
    up_part = (
        lax.dot_general(row_block, pair_weights[1], numbers, preferred_element_type=jnp.float32)
        + bias_part[1]
    )
    return activate(gate_part, up_part)


def routed_body(
    attn_out,
    out_weight,
    out_bias,
    residual_in,
    norm_gain,
    router_weight,
    router_bias,
    expert_ids,
    filled_rows,
    gate_up,
    gate_up_bias,
    down_weight,
    down_bias,
    next_gain,
):
    local_count = gate_up.shape[0]
    model_width = residual_in.shape[1]
    tok_rows = residual_in.shape[0]
    top_count = expert_ids.shape[1]
    experts_all = local_count * lax.axis_size("expert")
    capacity = 2 * tok_rows * top_count // experts_all
    row_block = attn_out
    summed = lax.psum_scatter(
        jnp.dot(row_block, out_weight, preferred_element_type=jnp.float32).astype(jnp.bfloat16),
        "expert",
        scatter_dimension=0,
        tiled=True,
    ).astype(jnp.float32)
    hidden_state = residual_in.astype(jnp.float32) + summed + out_bias
    normed_in = normalize(hidden_state, norm_gain).astype(jnp.bfloat16)
    logits = jnp.dot(normed_in, router_weight, preferred_element_type=jnp.float32) + router_bias
    chosen = jnp.take_along_axis(logits, expert_ids, axis=1)
    route_probs = jax.nn.softmax(chosen, axis=-1)
    live_rows = jnp.arange(tok_rows, dtype=jnp.int32) < filled_rows[0]
    route_weights = route_probs * live_rows[:, None].astype(jnp.float32)
    flat_ids = expert_ids.reshape(-1)
    onehot = (flat_ids[:, None] == jnp.arange(experts_all, dtype=jnp.int32)[None, :]).astype(
        jnp.int32
    )
    before = jnp.cumsum(onehot, axis=0) - onehot
    slot_ids = flat_ids * capacity + jnp.sum(before * onehot, axis=1)
    placing = (
        jnp.arange(experts_all * capacity, dtype=jnp.int32)[:, None] == slot_ids[None, :]
    ).astype(jnp.bfloat16)
    repeated = jnp.repeat(normed_in, top_count, axis=0)
    outgoing = jnp.dot(placing, repeated, preferred_element_type=jnp.float32).astype(jnp.bfloat16)
    outgoing = outgoing.reshape(experts_all, capacity, model_width)
    arrived = lax.all_to_all(outgoing, "expert", split_axis=0, concat_axis=0, tiled=True)
    arrived = arrived.reshape(-1, local_count, capacity, model_width)
    row_block = arrived[:, 0].reshape(-1, model_width)
    bias_pair = gate_up_bias[0]
    hidden = hidden_units(
        row_block, lax.all_gather(gate_up[0], "dp", axis=1, tiled=True), bias_pair
    )
    summed_rows = jnp.dot(
        hidden,
        lax.all_gather(down_weight[0], "dp", axis=0, tiled=True),
        preferred_element_type=jnp.float32,
    )
    results = [(summed_rows + down_bias[0]).astype(jnp.bfloat16).reshape(-1, capacity, model_width)]
    answered = jnp.stack(results, axis=1).reshape(-1, capacity, model_width)
    returned = lax.all_to_all(answered, "expert", split_axis=0, concat_axis=0, tiled=True)
    returned = returned.reshape(experts_all * capacity, model_width)
    picked = returned[slot_ids].astype(jnp.float32).reshape(tok_rows, top_count, model_width)
    mixture = jnp.sum(picked * route_weights[:, :, None], axis=1)
    stream_full = hidden_state + mixture
    return (
        stream_full.astype(jnp.bfloat16),
        normalize(stream_full, next_gain).astype(jnp.bfloat16),
    )


def dense_body(
    attn_out,
    out_weight,
    out_bias,
    residual_in,
    norm_gain,
    router_weight,
    router_bias,
    expert_ids,
    filled_rows,
    gate_up,
    gate_up_bias,
    down_weight,
    down_bias,
    next_gain,
):
    tok_rows = residual_in.shape[0]
    experts_all = gate_up.shape[0] * lax.axis_size("expert")
    hidden_rows = gate_up.shape[2]
    everyone = ("dp", "expert")
    summed = lax.psum_scatter(
        jnp.dot(attn_out, out_weight, preferred_element_type=jnp.float32).astype(jnp.bfloat16),
        "expert",
        scatter_dimension=0,
        tiled=True,
    ).astype(jnp.float32)
    hidden_state = residual_in.astype(jnp.float32) + summed + out_bias
    normed_in = normalize(hidden_state, norm_gain).astype(jnp.bfloat16)
    rows_all = lax.all_gather(normed_in, everyone, axis=0, tiled=True)
    logits = jnp.dot(normed_in, router_weight, preferred_element_type=jnp.float32) + router_bias
    hits = expert_ids[:, :, None] == jnp.arange(experts_all, dtype=jnp.int32)
    chosen = jnp.sum(jnp.where(hits, logits[:, None, :], 0.0), axis=-1)
    route_probs = jax.nn.softmax(chosen, axis=-1)
    live_rows = jnp.arange(tok_rows, dtype=jnp.int32) < filled_rows[0]
    route_weights = route_probs * live_rows[:, None].astype(jnp.float32)
    spread = jnp.sum(jnp.where(hits, route_weights[:, :, None], 0.0), axis=1)
    spread_all = lax.all_gather(spread, everyone, axis=0, tiled=True)
    mine = lax.dynamic_slice_in_dim(spread_all, lax.axis_index("expert"), 1, axis=1)
    dp_index = lax.axis_index("dp")
    bias_pair = lax.dynamic_slice_in_dim(
        gate_up_bias[0], dp_index * hidden_rows, hidden_rows, axis=1
    )
    hidden = hidden_units(rows_all, gate_up[0], bias_pair)
    part = jnp.dot(hidden, down_weight[0], preferred_element_type=jnp.float32)
    part = part + jnp.where(dp_index == 0, down_bias[0], 0.0)
    mixture = lax.psum_scatter(
        (part * mine).astype(jnp.bfloat16), everyone, scatter_dimension=0, tiled=True
    ).astype(jnp.float32)
    stream_full = hidden_state + mixture
    return (
        stream_full.astype(jnp.bfloat16),
        normalize(stream_full, next_gain).astype(jnp.bfloat16),
    )


def body(*arrays):
    residual_in, gate_up, down_weight = arrays[3], arrays[9], arrays[11]
    dp_size, expert_size = lax.axis_size("dp"), lax.axis_size("expert")
    token_rows = residual_in.shape[0] * dp_size * expert_size
    weight_rows = dp_size * (2 * gate_up.shape[2] + down_weight.shape[1])
    if gate_up.shape[0] == 1 and 2 * token_rows <= weight_rows:
        return dense_body(*arrays)
    return routed_body(*arrays)


def solution(mesh):
    return jax.shard_map(
        body,
        mesh=mesh,
        in_specs=(
            P("dp", "expert"),
            P("expert", None),
            P(),
            P(("dp", "expert"), None),
            P(),
            P(),
            P(),
            P(("dp", "expert"), None),
            P(("dp", "expert")),
            P("expert", None, "dp", None),
            P("expert", None, None),
            P("expert", "dp", None),
            P("expert", None),
            P(),
        ),
        out_specs=(P(("dp", "expert"), None), P(("dp", "expert"), None)),
        check_vma=False,
    )
```

```python
import functools

import jax
import jax.numpy as jnp
from jax import lax
from jax.experimental import pallas as pl
from jax.experimental.pallas import tpu as pltpu
from jax.sharding import PartitionSpec as P

EPS = 1e-05
LIMIT = 7.0
ALPHA = 1.702


def normalize(values, gain):
    return values * lax.rsqrt(jnp.mean(values * values, axis=-1, keepdims=True) + EPS) * gain


def activate(gate_part, up_part):
    gate_part = jnp.minimum(gate_part, LIMIT)
    up_part = jnp.clip(up_part, -LIMIT, LIMIT)
    return ((up_part + 1.0) * gate_part * jax.nn.sigmoid(ALPHA * gate_part)).astype(jnp.bfloat16)


def hidden_units(row_block, pair_weights, bias_part):
    numbers = (((1,), (1,)), ((), ()))
    gate_part = (
        lax.dot_general(row_block, pair_weights[0], numbers, preferred_element_type=jnp.float32)
        + bias_part[0]
    )
    up_part = (
        lax.dot_general(row_block, pair_weights[1], numbers, preferred_element_type=jnp.float32)
        + bias_part[1]
    )
    return activate(gate_part, up_part)


def routed_body(
    attn_out,
    out_weight,
    out_bias,
    residual_in,
    norm_gain,
    router_weight,
    router_bias,
    expert_ids,
    filled_rows,
    gate_up,
    gate_up_bias,
    down_weight,
    down_bias,
    next_gain,
):
    local_count = gate_up.shape[0]
    model_width = residual_in.shape[1]
    tok_rows = residual_in.shape[0]
    top_count = expert_ids.shape[1]
    experts_all = local_count * lax.axis_size("expert")
    capacity = 2 * tok_rows * top_count // experts_all
    row_block = attn_out
    summed = lax.psum_scatter(
        jnp.dot(row_block, out_weight, preferred_element_type=jnp.float32).astype(jnp.bfloat16),
        "expert",
        scatter_dimension=0,
        tiled=True,
    ).astype(jnp.float32)
    hidden_state = residual_in.astype(jnp.float32) + summed + out_bias
    normed_in = normalize(hidden_state, norm_gain).astype(jnp.bfloat16)
    logits = jnp.dot(normed_in, router_weight, preferred_element_type=jnp.float32) + router_bias
    chosen = jnp.take_along_axis(logits, expert_ids, axis=1)
    route_probs = jax.nn.softmax(chosen, axis=-1)
    live_rows = jnp.arange(tok_rows, dtype=jnp.int32) < filled_rows[0]
    route_weights = route_probs * live_rows[:, None].astype(jnp.float32)
    flat_ids = expert_ids.reshape(-1)
    onehot = (flat_ids[:, None] == jnp.arange(experts_all, dtype=jnp.int32)[None, :]).astype(
        jnp.int32
    )
    before = jnp.cumsum(onehot, axis=0) - onehot
    slot_ids = flat_ids * capacity + jnp.sum(before * onehot, axis=1)
    placing = (
        jnp.arange(experts_all * capacity, dtype=jnp.int32)[:, None] == slot_ids[None, :]
    ).astype(jnp.bfloat16)
    repeated = jnp.repeat(normed_in, top_count, axis=0)
    outgoing = jnp.dot(placing, repeated, preferred_element_type=jnp.float32).astype(jnp.bfloat16)
    outgoing = outgoing.reshape(experts_all, capacity, model_width)
    arrived = lax.all_to_all(outgoing, "expert", split_axis=0, concat_axis=0, tiled=True)
    arrived = arrived.reshape(-1, local_count, capacity, model_width)
    row_block = arrived[:, 0].reshape(-1, model_width)
    bias_pair = gate_up_bias[0]
    hidden = hidden_units(
        row_block, lax.all_gather(gate_up[0], "dp", axis=1, tiled=True), bias_pair
    )
    summed_rows = jnp.dot(
        hidden,
        lax.all_gather(down_weight[0], "dp", axis=0, tiled=True),
        preferred_element_type=jnp.float32,
    )
    results = [(summed_rows + down_bias[0]).astype(jnp.bfloat16).reshape(-1, capacity, model_width)]
    answered = jnp.stack(results, axis=1).reshape(-1, capacity, model_width)
    returned = lax.all_to_all(answered, "expert", split_axis=0, concat_axis=0, tiled=True)
    returned = returned.reshape(experts_all * capacity, model_width)
    picked = returned[slot_ids].astype(jnp.float32).reshape(tok_rows, top_count, model_width)
    mixture = jnp.sum(picked * route_weights[:, :, None], axis=1)
    stream_full = hidden_state + mixture
    return (
        stream_full.astype(jnp.bfloat16),
        normalize(stream_full, next_gain).astype(jnp.bfloat16),
    )


def place():
    z, e = lax.axis_index("dp"), lax.axis_index("expert")
    y, x, core = e // 4, (e // 2) % 2, e % 2
    at = lambda yy, xx, cc: yy * 4 + xx * 2 + cc
    return dict(
        z=z, e=e, y=y, x=x, core=core,
        s=at(y, x, 1 - core), xn=at(y, 1 - x, core), yn=at(1 - y, x, core),
        dn=at(1 - y, 1 - x, core),
    )


def remote(src, dst, send_sem, recv_sem, device):
    return pltpu.make_async_remote_copy(
        src_ref=src, dst_ref=dst, send_sem=send_sem, recv_sem=recv_sem,
        device_id=device, device_id_type=pl.DeviceIdType.MESH,
    )


def greet(devices):
    barrier = pltpu.get_barrier_semaphore()
    for device in devices:
        pl.semaphore_signal(
            barrier, inc=1, device_id=device, device_id_type=pl.DeviceIdType.MESH
        )
    pl.semaphore_wait(barrier, len(devices))


class PlaneSum:
    def __init__(self, here, parts, paired, from_x, from_y, last, send, recv, sent):
        self.here, self.parts, self.paired = here, parts, paired
        self.from_x, self.from_y, self.last = from_x, from_y, last
        self.send, self.recv, self.sent = send, recv, sent
        self.half = parts.shape[4] // 2

    def put(self, src, dst, k, lane, to):
        copy = remote(
            src, dst, self.send.at[k, lane], self.recv.at[k, lane], (self.here["z"], self.here[to])
        )
        copy.start()
        self.sent.append(copy)

    def take(self, dst, k, lane, to):
        remote(
            dst, dst, self.send.at[k, lane], self.recv.at[k, lane], (self.here["z"], self.here[to])
        ).wait_recv()

    def pair(self, k):
        self.put(self.parts.at[k, 1 - self.here["core"]], self.paired.at[k], k, 0, "s")

    def first(self, k):
        core, x, y, half = self.here["core"], self.here["x"], self.here["y"], self.half
        self.take(self.paired.at[k], k, 0, "s")

        @pl.loop(0, 4)
        def _(i):
            yy, xx = i // 2, i % 2
            self.parts[k, core, yy, xx] = (
                self.parts[k, core, yy, xx].astype(jnp.float32)
                + self.paired[k, yy, xx].astype(jnp.float32)
            ).astype(jnp.bfloat16)

        low, high = pl.ds(0, half), pl.ds(half, half)
        self.put(self.parts.at[k, core, :, 1 - x, low], self.from_x.at[k], k, 1, "xn")
        self.put(self.parts.at[k, core, 1 - y, :, high], self.from_y.at[k], k, 2, "yn")

    def second(self, k):
        core, x, y, half = self.here["core"], self.here["x"], self.here["y"], self.half
        low, high = pl.ds(0, half), pl.ds(half, half)

        def add(yy, xx, rows, more):
            self.parts[k, core, yy, xx, rows] = (
                self.parts[k, core, yy, xx, rows].astype(jnp.float32) + more.astype(jnp.float32)
            ).astype(jnp.bfloat16)

        self.take(self.from_x.at[k], k, 1, "xn")
        add(1 - y, x, low, self.from_x[k, 1 - y])
        self.put(self.parts.at[k, core, 1 - y, x, low], self.last.at[k, low], k, 3, "yn")
        self.take(self.from_y.at[k], k, 2, "yn")
        add(y, 1 - x, high, self.from_y[k, 1 - x])
        self.put(self.parts.at[k, core, y, 1 - x, high], self.last.at[k, high], k, 4, "xn")

    def third(self, k):
        core, x, y, half = self.here["core"], self.here["x"], self.here["y"], self.half
        low, high = pl.ds(0, half), pl.ds(half, half)
        self.take(self.last.at[k, low], k, 3, "yn")
        self.take(self.last.at[k, high], k, 4, "xn")
        own = self.parts[k, core, y, x].astype(jnp.float32) + self.last[k].astype(jnp.float32)
        more = jnp.concatenate([self.from_x[k, y], self.from_y[k, x]], axis=0)
        return own + more.astype(jnp.float32)


def plane_scratch(groups, rows, width):
    return [
        pltpu.VMEM((groups, 2, 2, 2, rows, width), jnp.bfloat16),
        pltpu.VMEM((groups, 2, 2, rows, width), jnp.bfloat16),
        pltpu.VMEM((groups, 2, rows // 2, width), jnp.bfloat16),
        pltpu.VMEM((groups, 2, rows // 2, width), jnp.bfloat16),
        pltpu.VMEM((groups, rows, width), jnp.bfloat16),
        pltpu.SemaphoreType.DMA((groups, 5)),
        pltpu.SemaphoreType.DMA((groups, 5)),
    ]


def projection_kernel(attn, weight, out, parts, paired, from_x, from_y, last, send, recv):
    here = place()
    rows = attn.shape[2]
    greet([(here["z"], here[name]) for name in ("s", "xn", "yn")])
    sent = []
    plane = PlaneSum(here, parts, paired, from_x, from_y, last, send, recv, sent)
    for turn in range(2):
        core = 1 - here["core"] if turn == 0 else here["core"]
        block = attn[:, core].reshape(4 * rows, attn.shape[3])
        result = jnp.dot(block, weight[...], preferred_element_type=jnp.float32).astype(jnp.bfloat16)
        for i in range(4):
            parts[0, core, i // 2, i % 2] = result[i * rows : (i + 1) * rows]
        if turn == 0:
            plane.pair(0)
    plane.first(0)
    plane.second(0)
    out[...] = plane.third(0)
    for copy in sent:
        copy.wait_send()


def project(attn_out, out_weight):
    tokens, features = attn_out.shape
    width = out_weight.shape[1]
    rows = tokens // 8
    vmem = pl.BlockSpec(memory_space=pltpu.VMEM)
    return pl.pallas_call(
        projection_kernel,
        out_shape=jax.ShapeDtypeStruct((rows, width), jnp.float32),
        in_specs=[vmem, vmem],
        out_specs=vmem,
        scratch_shapes=plane_scratch(1, rows, width),
        compiler_params=pltpu.CompilerParams(
            collective_id=0, has_side_effects=True, vmem_limit_bytes=48 * 1024 * 1024
        ),
    )(attn_out.reshape(4, 2, rows, features), out_weight)


def experts_kernel(
    groups, block, gate_up, bias_pair, down, down_bias, hidden_state, next_gain,
    stream, normed_next,
    tok, gu, dw, acc, zin, zout, gsend, grecv, zsend, zrecv, lsem,
    parts, paired, from_x, from_y, last, send, recv,
):
    here = place()
    z, e, core = here["z"], here["e"], here["core"]
    rows, width = hidden_state.shape
    half = rows // 2
    low, high = pl.ds(0, half), pl.ds(half, half)
    loads = [
        pltpu.make_async_copy(block, tok.at[z, e], lsem.at[0]),
        pltpu.make_async_copy(gate_up, gu, lsem.at[1]),
        pltpu.make_async_copy(down, dw, lsem.at[2]),
    ]
    for load in loads:
        load.start()
    ring = [(lax.rem(z + j, groups), e) for j in range(1, groups)]
    greet([(z, here[name]) for name in ("s", "xn", "yn")] + ring)
    sent = []
    plane = PlaneSum(here, parts, paired, from_x, from_y, last, send, recv, sent)
    group = [lax.rem(z + groups - k, groups) for k in range(groups)]

    def put(src, dst, k, lane, device):
        copy = remote(src, dst, gsend.at[k, lane], grecv.at[k, lane], device)
        copy.start()
        sent.append(copy)

    def take(dst, k, lane, device):
        remote(dst, dst, gsend.at[k, lane], grecv.at[k, lane], device).wait_recv()

    sib, to_x, to_y = (z, here["s"]), (z, here["xn"]), (z, here["yn"])

    def enter(k):
        g = group[k]
        if k > 0:
            take(tok.at[g, e], k, 0, ring[k - 1])
        src = block if k == 0 else tok.at[g, e]
        put(src, tok.at[g, e], k, 1, to_x)
        put(src, tok.at[g, e], k, 2, to_y)
        if k == 0:
            for j in range(1, groups):
                put(block, tok.at[z, e], j, 0, ring[j - 1])
        put(src, tok.at[g, e], k, 5, sib)

    def across(k):
        g, xn, yn = group[k], here["xn"], here["yn"]
        take(tok.at[g, xn], k, 1, to_x)
        put(tok.at[g, xn, low], tok.at[g, xn, low], k, 3, to_y)
        put(tok.at[g, xn], tok.at[g, xn], k, 6, sib)
        take(tok.at[g, yn], k, 2, to_y)
        put(tok.at[g, yn, high], tok.at[g, yn, high], k, 4, to_x)
        put(tok.at[g, yn], tok.at[g, yn], k, 7, sib)

    def corner(k):
        g, dn = group[k], here["dn"]
        take(tok.at[g, dn, low], k, 3, to_y)
        take(tok.at[g, dn, high], k, 4, to_x)
        put(tok.at[g, dn], tok.at[g, dn], k, 8, sib)

    def compute(k):
        g = group[k]
        for lane, name in ((5, "e"), (6, "xn"), (7, "yn"), (8, "dn")):
            other = here[name] + 1 - 2 * core
            take(tok.at[g, other], k, lane, sib)
        if k == 0:
            for load in loads:
                load.wait()

        @pl.loop(0, 2)
        def _(m):
            mine = pl.ds(m * 4, 4)
            values = tok[g, mine, :, :width].reshape(4 * rows, width)
            hidden = hidden_units(values, (gu[0], gu[1]), (bias_pair[0:1], bias_pair[1:2]))
            part = jnp.dot(hidden, dw[...], preferred_element_type=jnp.float32)
            part = part + jnp.where(z == 0, down_bias[...], 0.0)
            tail = tok[g, mine, :, tok.shape[3] - 128 :].reshape(4 * rows, 128)
            lane = lax.broadcasted_iota(jnp.int32, tail.shape, 1) - 64
            picked = (lane == e) | (lane == e + 8)
            share = jnp.sum(
                jnp.where(picked, tail.astype(jnp.float32), 0.0), axis=1, keepdims=True
            )
            part = (part * share).astype(jnp.bfloat16)
            for i in range(4):
                parts[k, i % 2, m, i // 2] = part[i * rows : (i + 1) * rows]

        plane.pair(k)

    def leave(k):
        total = plane.third(k)
        if k == 0:
            acc[...] = total
            return
        zout[k - 1] = total.astype(jnp.bfloat16)
        copy = remote(
            zout.at[k - 1], zin.at[k - 1], zsend.at[k - 1], zrecv.at[k - 1], (group[k], e)
        )
        copy.start()
        sent.append(copy)

    for step in range(groups + 8):
        for delay, stage in (
            (0, enter), (1, across), (2, corner), (6, leave),
            (5, plane.second), (4, plane.first), (3, compute),
        ):
            if 0 <= step - delay < groups:
                stage(step - delay)
    full = hidden_state[...] + acc[...]
    for k in range(groups - 1):
        remote(zin.at[k], zin.at[k], zsend.at[k], zrecv.at[k], (group[k + 1], e)).wait_recv()
        full = full + zin[k].astype(jnp.float32)
    stream[...] = full.astype(jnp.bfloat16)
    normed_next[...] = normalize(full, next_gain[...]).astype(jnp.bfloat16)
    for copy in sent:
        copy.wait_send()


def experts(block, gate_up, bias_pair, down, down_bias, hidden_state, next_gain):
    groups = lax.axis_size("dp")
    rows, width = hidden_state.shape
    wide = block.shape[1]
    vmem = pl.BlockSpec(memory_space=pltpu.VMEM)
    anywhere = pl.BlockSpec(memory_space=pl.ANY)
    result = jax.ShapeDtypeStruct((rows, width), jnp.bfloat16)
    return pl.pallas_call(
        functools.partial(experts_kernel, groups),
        out_shape=(result, result),
        in_specs=[vmem, anywhere, vmem, anywhere, vmem, vmem, vmem],
        out_specs=(vmem, vmem),
        scratch_shapes=[
            pltpu.VMEM((groups, 8, rows, wide), jnp.bfloat16),
            pltpu.VMEM(gate_up.shape, jnp.bfloat16),
            pltpu.VMEM(down.shape, jnp.bfloat16),
            pltpu.VMEM((rows, width), jnp.float32),
            pltpu.VMEM((groups - 1, rows, width), jnp.bfloat16),
            pltpu.VMEM((groups - 1, rows, width), jnp.bfloat16),
            pltpu.SemaphoreType.DMA((groups, 9)),
            pltpu.SemaphoreType.DMA((groups, 9)),
            pltpu.SemaphoreType.DMA((groups - 1,)),
            pltpu.SemaphoreType.DMA((groups - 1,)),
            pltpu.SemaphoreType.DMA((3,)),
        ]
        + plane_scratch(groups, rows, width),
        compiler_params=pltpu.CompilerParams(
            collective_id=1, has_side_effects=True, vmem_limit_bytes=60 * 1024 * 1024
        ),
    )(block, gate_up, bias_pair, down, down_bias, hidden_state, next_gain)


def dense_body(
    attn_out,
    out_weight,
    out_bias,
    residual_in,
    norm_gain,
    router_weight,
    router_bias,
    expert_ids,
    filled_rows,
    gate_up,
    gate_up_bias,
    down_weight,
    down_bias,
    next_gain,
):
    tok_rows = residual_in.shape[0]
    experts_all = gate_up.shape[0] * lax.axis_size("expert")
    hidden_rows = gate_up.shape[2]
    summed = project(attn_out, out_weight)
    hidden_state = residual_in.astype(jnp.float32) + summed + out_bias
    normed_in = normalize(hidden_state, norm_gain).astype(jnp.bfloat16)
    logits = jnp.dot(normed_in, router_weight, preferred_element_type=jnp.float32) + router_bias
    hits = expert_ids[:, :, None] == jnp.arange(experts_all, dtype=jnp.int32)
    chosen = jnp.sum(jnp.where(hits, logits[:, None, :], 0.0), axis=-1)
    route_probs = jax.nn.softmax(chosen, axis=-1)
    live_rows = jnp.arange(tok_rows, dtype=jnp.int32) < filled_rows[0]
    route_weights = route_probs * live_rows[:, None].astype(jnp.float32)
    spread = jnp.sum(jnp.where(hits, route_weights[:, :, None], 0.0), axis=1)
    coarse = lax.reduce_precision(spread, 8, 7)
    spare = 64 - 2 * experts_all
    block = jnp.concatenate(
        [
            normed_in,
            coarse.astype(jnp.bfloat16),
            (spread - coarse).astype(jnp.bfloat16),
            jnp.zeros((tok_rows, spare), jnp.bfloat16),
        ],
        axis=1,
    )
    bias_pair = lax.dynamic_slice_in_dim(
        gate_up_bias[0], lax.axis_index("dp") * hidden_rows, hidden_rows, axis=1
    )
    return experts(
        block, gate_up[0], bias_pair, down_weight[0], down_bias, hidden_state, next_gain[None]
    )


def body(*arrays):
    residual_in, gate_up, down_weight = arrays[3], arrays[9], arrays[11]
    dp_size, expert_size = lax.axis_size("dp"), lax.axis_size("expert")
    token_rows = residual_in.shape[0] * dp_size * expert_size
    weight_rows = dp_size * (2 * gate_up.shape[2] + down_weight.shape[1])
    if gate_up.shape[0] == 1 and expert_size == 8 and 2 * token_rows <= weight_rows:
        return dense_body(*arrays)
    return routed_body(*arrays)


def solution(mesh):
    return jax.shard_map(
        body,
        mesh=mesh,
        in_specs=(
            P("dp", "expert"),
            P("expert", None),
            P(),
            P(("dp", "expert"), None),
            P(),
            P(),
            P(),
            P(("dp", "expert"), None),
            P(("dp", "expert")),
            P("expert", None, "dp", None),
            P("expert", None, None),
            P("expert", "dp", None),
            P("expert", None),
            P(),
        ),
        out_specs=(P(("dp", "expert"), None), P(("dp", "expert"), None)),
        check_vma=False,
    )
```

```python
import functools

import jax
import jax.numpy as jnp
from jax import lax
from jax.experimental import pallas as pl
from jax.experimental.pallas import tpu as pltpu
from jax.sharding import PartitionSpec as P

EPS = 1e-05
LIMIT = 7.0
ALPHA = 1.702


def normalize(values, gain):
    return values * lax.rsqrt(jnp.mean(values * values, axis=-1, keepdims=True) + EPS) * gain


def activate(gate_part, up_part):
    gate_part = jnp.minimum(gate_part, LIMIT)
    up_part = jnp.clip(up_part, -LIMIT, LIMIT)
    return ((up_part + 1.0) * gate_part * jax.nn.sigmoid(ALPHA * gate_part)).astype(jnp.bfloat16)


def hidden_units(row_block, pair_weights, bias_part):
    numbers = (((1,), (1,)), ((), ()))
    gate_part = (
        lax.dot_general(row_block, pair_weights[0], numbers, preferred_element_type=jnp.float32)
        + bias_part[0]
    )
    up_part = (
        lax.dot_general(row_block, pair_weights[1], numbers, preferred_element_type=jnp.float32)
        + bias_part[1]
    )
    return activate(gate_part, up_part)


def routed_body(
    attn_out,
    out_weight,
    out_bias,
    residual_in,
    norm_gain,
    router_weight,
    router_bias,
    expert_ids,
    filled_rows,
    gate_up,
    gate_up_bias,
    down_weight,
    down_bias,
    next_gain,
):
    local_count = gate_up.shape[0]
    model_width = residual_in.shape[1]
    tok_rows = residual_in.shape[0]
    top_count = expert_ids.shape[1]
    experts_all = local_count * lax.axis_size("expert")
    capacity = 2 * tok_rows * top_count // experts_all
    row_block = attn_out
    summed = lax.psum_scatter(
        jnp.dot(row_block, out_weight, preferred_element_type=jnp.float32).astype(jnp.bfloat16),
        "expert",
        scatter_dimension=0,
        tiled=True,
    ).astype(jnp.float32)
    hidden_state = residual_in.astype(jnp.float32) + summed + out_bias
    normed_in = normalize(hidden_state, norm_gain).astype(jnp.bfloat16)
    logits = jnp.dot(normed_in, router_weight, preferred_element_type=jnp.float32) + router_bias
    chosen = jnp.take_along_axis(logits, expert_ids, axis=1)
    route_probs = jax.nn.softmax(chosen, axis=-1)
    live_rows = jnp.arange(tok_rows, dtype=jnp.int32) < filled_rows[0]
    route_weights = route_probs * live_rows[:, None].astype(jnp.float32)
    flat_ids = expert_ids.reshape(-1)
    onehot = (flat_ids[:, None] == jnp.arange(experts_all, dtype=jnp.int32)[None, :]).astype(
        jnp.int32
    )
    before = jnp.cumsum(onehot, axis=0) - onehot
    slot_ids = flat_ids * capacity + jnp.sum(before * onehot, axis=1)
    placing = (
        jnp.arange(experts_all * capacity, dtype=jnp.int32)[:, None] == slot_ids[None, :]
    ).astype(jnp.bfloat16)
    repeated = jnp.repeat(normed_in, top_count, axis=0)
    outgoing = jnp.dot(placing, repeated, preferred_element_type=jnp.float32).astype(jnp.bfloat16)
    outgoing = outgoing.reshape(experts_all, capacity, model_width)
    arrived = lax.all_to_all(outgoing, "expert", split_axis=0, concat_axis=0, tiled=True)
    arrived = arrived.reshape(-1, local_count, capacity, model_width)
    row_block = arrived[:, 0].reshape(-1, model_width)
    bias_pair = gate_up_bias[0]
    hidden = hidden_units(
        row_block, lax.all_gather(gate_up[0], "dp", axis=1, tiled=True), bias_pair
    )
    summed_rows = jnp.dot(
        hidden,
        lax.all_gather(down_weight[0], "dp", axis=0, tiled=True),
        preferred_element_type=jnp.float32,
    )
    results = [(summed_rows + down_bias[0]).astype(jnp.bfloat16).reshape(-1, capacity, model_width)]
    answered = jnp.stack(results, axis=1).reshape(-1, capacity, model_width)
    returned = lax.all_to_all(answered, "expert", split_axis=0, concat_axis=0, tiled=True)
    returned = returned.reshape(experts_all * capacity, model_width)
    picked = returned[slot_ids].astype(jnp.float32).reshape(tok_rows, top_count, model_width)
    mixture = jnp.sum(picked * route_weights[:, :, None], axis=1)
    stream_full = hidden_state + mixture
    return (
        stream_full.astype(jnp.bfloat16),
        normalize(stream_full, next_gain).astype(jnp.bfloat16),
    )


def place():
    z, e = lax.axis_index("dp"), lax.axis_index("expert")
    y, x, core = e // 4, (e // 2) % 2, e % 2
    at = lambda yy, xx, cc: yy * 4 + xx * 2 + cc
    return dict(
        z=z, e=e, y=y, x=x, core=core,
        s=at(y, x, 1 - core), xn=at(y, 1 - x, core), yn=at(1 - y, x, core),
        dn=at(1 - y, 1 - x, core),
    )


def remote(src, dst, send_sem, recv_sem, device):
    return pltpu.make_async_remote_copy(
        src_ref=src, dst_ref=dst, send_sem=send_sem, recv_sem=recv_sem,
        device_id=device, device_id_type=pl.DeviceIdType.MESH,
    )


def greet(devices):
    barrier = pltpu.get_barrier_semaphore()
    for device in devices:
        pl.semaphore_signal(
            barrier, inc=1, device_id=device, device_id_type=pl.DeviceIdType.MESH
        )
    pl.semaphore_wait(barrier, len(devices))


class PlaneSum:
    def __init__(self, here, parts, paired, from_x, from_y, last, send, recv, sent):
        self.here, self.parts, self.paired = here, parts, paired
        self.from_x, self.from_y, self.last = from_x, from_y, last
        self.send, self.recv, self.sent = send, recv, sent
        self.half = parts.shape[4] // 2

    def put(self, src, dst, k, lane, to):
        copy = remote(
            src, dst, self.send.at[k, lane], self.recv.at[k, lane], (self.here["z"], self.here[to])
        )
        copy.start()
        self.sent.append(copy)

    def take(self, dst, k, lane, to):
        remote(
            dst, dst, self.send.at[k, lane], self.recv.at[k, lane], (self.here["z"], self.here[to])
        ).wait_recv()

    def pair(self, k):
        self.put(self.parts.at[k, 1 - self.here["core"]], self.paired.at[k], k, 0, "s")

    def first(self, k):
        core, x, y, half = self.here["core"], self.here["x"], self.here["y"], self.half
        self.take(self.paired.at[k], k, 0, "s")

        @pl.loop(0, 4)
        def _(i):
            yy, xx = i // 2, i % 2
            self.parts[k, core, yy, xx] = (
                self.parts[k, core, yy, xx].astype(jnp.float32)
                + self.paired[k, yy, xx].astype(jnp.float32)
            ).astype(jnp.bfloat16)

        low, high = pl.ds(0, half), pl.ds(half, half)
        self.put(self.parts.at[k, core, :, 1 - x, low], self.from_x.at[k], k, 1, "xn")
        self.put(self.parts.at[k, core, 1 - y, :, high], self.from_y.at[k], k, 2, "yn")

    def second(self, k):
        core, x, y, half = self.here["core"], self.here["x"], self.here["y"], self.half
        low, high = pl.ds(0, half), pl.ds(half, half)

        def add(yy, xx, rows, more):
            self.parts[k, core, yy, xx, rows] = (
                self.parts[k, core, yy, xx, rows].astype(jnp.float32) + more.astype(jnp.float32)
            ).astype(jnp.bfloat16)

        self.take(self.from_x.at[k], k, 1, "xn")
        add(1 - y, x, low, self.from_x[k, 1 - y])
        self.put(self.parts.at[k, core, 1 - y, x, low], self.last.at[k, low], k, 3, "yn")
        self.take(self.from_y.at[k], k, 2, "yn")
        add(y, 1 - x, high, self.from_y[k, 1 - x])
        self.put(self.parts.at[k, core, y, 1 - x, high], self.last.at[k, high], k, 4, "xn")

    def third(self, k):
        core, x, y, half = self.here["core"], self.here["x"], self.here["y"], self.half
        low, high = pl.ds(0, half), pl.ds(half, half)
        self.take(self.last.at[k, low], k, 3, "yn")
        self.take(self.last.at[k, high], k, 4, "xn")
        own = self.parts[k, core, y, x].astype(jnp.float32) + self.last[k].astype(jnp.float32)
        more = jnp.concatenate([self.from_x[k, y], self.from_y[k, x]], axis=0)
        return own + more.astype(jnp.float32)


def plane_scratch(groups, rows, width):
    return [
        pltpu.VMEM((groups, 2, 2, 2, rows, width), jnp.bfloat16),
        pltpu.VMEM((groups, 2, 2, rows, width), jnp.bfloat16),
        pltpu.VMEM((groups, 2, rows // 2, width), jnp.bfloat16),
        pltpu.VMEM((groups, 2, rows // 2, width), jnp.bfloat16),
        pltpu.VMEM((groups, rows, width), jnp.bfloat16),
        pltpu.SemaphoreType.DMA((groups, 5)),
        pltpu.SemaphoreType.DMA((groups, 5)),
    ]


CHUNKS = 2


def projection_kernel(
    attn, weight, out, held, lsem, parts, paired, from_x, from_y, last, send, recv
):
    here = place()
    rows = attn.shape[2] // CHUNKS
    load = pltpu.make_async_copy(weight, held, lsem)
    load.start()
    greet([(here["z"], here[name]) for name in ("s", "xn", "yn")])
    sent = []
    plane = PlaneSum(here, parts, paired, from_x, from_y, last, send, recv, sent)
    load.wait()

    def multiply(chunk, core):
        block = attn[:, core, chunk * rows : (chunk + 1) * rows].reshape(4 * rows, attn.shape[3])
        result = jnp.dot(block, held[...], preferred_element_type=jnp.float32).astype(jnp.bfloat16)
        for i in range(4):
            parts[chunk, core, i // 2, i % 2] = result[i * rows : (i + 1) * rows]

    for chunk in range(CHUNKS):
        multiply(chunk, 1 - here["core"])
        plane.pair(chunk)
    for chunk in range(CHUNKS):
        multiply(chunk, here["core"])
        plane.first(chunk)
    for chunk in range(CHUNKS):
        plane.second(chunk)
    for chunk in range(CHUNKS):
        out[chunk * rows : (chunk + 1) * rows] = plane.third(chunk)
    for copy in sent:
        copy.wait_send()


def project(attn_out, out_weight):
    tokens, features = attn_out.shape
    width = out_weight.shape[1]
    rows = tokens // 8
    vmem = pl.BlockSpec(memory_space=pltpu.VMEM)
    return pl.pallas_call(
        projection_kernel,
        out_shape=jax.ShapeDtypeStruct((rows, width), jnp.float32),
        in_specs=[vmem, pl.BlockSpec(memory_space=pl.ANY)],
        out_specs=vmem,
        scratch_shapes=[pltpu.VMEM(out_weight.shape, jnp.bfloat16), pltpu.SemaphoreType.DMA]
        + plane_scratch(CHUNKS, rows // CHUNKS, width),
        compiler_params=pltpu.CompilerParams(
            collective_id=0, has_side_effects=True, vmem_limit_bytes=60 * 1024 * 1024
        ),
    )(attn_out.reshape(4, 2, rows, features), out_weight)


def experts_kernel(
    groups, block, gate_up, bias_all, down, down_bias, hidden_state, full_out,
    tok, bias_pair, gu, dw, acc, zin, zout, gsend, grecv, zsend, zrecv, lsem,
    parts, paired, from_x, from_y, last, send, recv,
):
    here = place()
    z, e, core = here["z"], here["e"], here["core"]
    rows, width = hidden_state.shape
    half = rows // 2
    low, high = pl.ds(0, half), pl.ds(half, half)
    loads = [
        pltpu.make_async_copy(block, tok.at[z, e], lsem.at[0]),
        pltpu.make_async_copy(gate_up, gu, lsem.at[1]),
        pltpu.make_async_copy(down, dw, lsem.at[2]),
    ]
    for load in loads:
        load.start()
    units = bias_pair.shape[1]
    bias_pair[...] = sum(
        jnp.where(z == j, bias_all[:, j * units : (j + 1) * units], 0.0) for j in range(groups)
    )
    group = [z] + [z + j - 2 * sum(b * ((z // b) % 2) for b in (1, 2, 4) if j & b) for j in range(1, groups)]
    ring = [(group[j], e) for j in range(1, groups)]
    greet([(z, here[name]) for name in ("s", "xn", "yn")] + ring)
    sent = []
    plane = PlaneSum(here, parts, paired, from_x, from_y, last, send, recv, sent)

    def put(src, dst, k, lane, device):
        copy = remote(src, dst, gsend.at[k, lane], grecv.at[k, lane], device)
        copy.start()
        sent.append(copy)

    def take(dst, k, lane, device):
        remote(dst, dst, gsend.at[k, lane], grecv.at[k, lane], device).wait_recv()

    sib, to_x, to_y = (z, here["s"]), (z, here["xn"]), (z, here["yn"])

    def enter(k):
        g = group[k]
        if k > 0:
            take(tok.at[g, e], k, 0, ring[k - 1])
        src = block if k == 0 else tok.at[g, e]
        put(src, tok.at[g, e], k, 1, to_x)
        put(src, tok.at[g, e], k, 2, to_y)
        for j in ((1, 2), (3,))[k] if k < 2 else ():
            put(block, tok.at[z, e], j, 0, ring[j - 1])
        put(src, tok.at[g, e], k, 5, sib)

    def across(k):
        g, xn, yn = group[k], here["xn"], here["yn"]
        take(tok.at[g, xn], k, 1, to_x)
        put(tok.at[g, xn, low], tok.at[g, xn, low], k, 3, to_y)
        put(tok.at[g, xn], tok.at[g, xn], k, 6, sib)
        take(tok.at[g, yn], k, 2, to_y)
        put(tok.at[g, yn, high], tok.at[g, yn, high], k, 4, to_x)
        put(tok.at[g, yn], tok.at[g, yn], k, 7, sib)

    def corner(k):
        g, dn = group[k], here["dn"]
        take(tok.at[g, dn, low], k, 3, to_y)
        take(tok.at[g, dn, high], k, 4, to_x)
        put(tok.at[g, dn], tok.at[g, dn], k, 8, sib)

    def compute(k):
        g = group[k]
        for lane, name in ((5, "e"), (6, "xn"), (7, "yn"), (8, "dn")):
            other = here[name] + 1 - 2 * core
            take(tok.at[g, other], k, lane, sib)
        if k == 0:
            for load in loads:
                load.wait()

        @pl.loop(0, 2)
        def _(m):
            mine = pl.ds(m * 4, 4)
            values = tok[g, mine, :, :width].reshape(4 * rows, width)
            hidden = hidden_units(values, (gu[0], gu[1]), (bias_pair[0:1], bias_pair[1:2]))
            part = jnp.dot(hidden, dw[...], preferred_element_type=jnp.float32)
            part = part + jnp.where(z == 0, down_bias[...], 0.0)
            tail = tok[g, mine, :, tok.shape[3] - 128 :].reshape(4 * rows, 128)
            lane = lax.broadcasted_iota(jnp.int32, tail.shape, 1) - 64
            picked = (lane == e) | (lane == e + 8)
            share = jnp.sum(
                jnp.where(picked, tail.astype(jnp.float32), 0.0), axis=1, keepdims=True
            )
            part = (part * share).astype(jnp.bfloat16)
            for i in range(4):
                parts[k, i % 2, m, i // 2] = part[i * rows : (i + 1) * rows]

        plane.pair(k)

    def leave(k):
        total = plane.third(k)
        if k == 0:
            acc[...] = total
            return
        zout[k - 1] = total.astype(jnp.bfloat16)
        copy = remote(
            zout.at[k - 1], zin.at[k - 1], zsend.at[k - 1], zrecv.at[k - 1], (group[k], e)
        )
        copy.start()
        sent.append(copy)

    for stage, k in (
        (enter, 0), (enter, 1), (across, 0), (enter, 2), (corner, 0), (across, 1),
        (enter, 3), (corner, 1), (across, 2), (compute, 0), (corner, 2), (across, 3),
        (compute, 1), (compute, 2), (corner, 3), (plane.first, 2), (compute, 3),
        (plane.second, 2), (plane.first, 3), (plane.first, 1), (plane.second, 3), (leave, 2),
        (plane.first, 0), (plane.second, 1), (leave, 3), (plane.second, 0), (leave, 1), (leave, 0),
    ):
        stage(k)
    full = hidden_state[...] + acc[...]
    for k in range(groups - 1):
        remote(zin.at[k], zin.at[k], zsend.at[k], zrecv.at[k], (group[k + 1], e)).wait_recv()
        full = full + zin[k].astype(jnp.float32)
    full_out[...] = full
    for copy in sent:
        copy.wait_send()


def experts(block, gate_up, bias_all, down, down_bias, hidden_state):
    groups = lax.axis_size("dp")
    rows, width = hidden_state.shape
    wide = block.shape[1]
    vmem = pl.BlockSpec(memory_space=pltpu.VMEM)
    anywhere = pl.BlockSpec(memory_space=pl.ANY)
    return pl.pallas_call(
        functools.partial(experts_kernel, groups),
        out_shape=jax.ShapeDtypeStruct((rows, width), jnp.float32),
        in_specs=[vmem, anywhere, vmem, anywhere, vmem, vmem],
        out_specs=vmem,
        scratch_shapes=[
            pltpu.VMEM((groups, 8, rows, wide), jnp.bfloat16),
            pltpu.VMEM(gate_up.shape[:2], jnp.float32),
            pltpu.VMEM(gate_up.shape, jnp.bfloat16),
            pltpu.VMEM(down.shape, jnp.bfloat16),
            pltpu.VMEM((rows, width), jnp.float32),
            pltpu.VMEM((groups - 1, rows, width), jnp.bfloat16),
            pltpu.VMEM((groups - 1, rows, width), jnp.bfloat16),
            pltpu.SemaphoreType.DMA((groups, 9)),
            pltpu.SemaphoreType.DMA((groups, 9)),
            pltpu.SemaphoreType.DMA((groups - 1,)),
            pltpu.SemaphoreType.DMA((groups - 1,)),
            pltpu.SemaphoreType.DMA((3,)),
        ]
        + plane_scratch(groups, rows, width),
        compiler_params=pltpu.CompilerParams(
            collective_id=1, has_side_effects=True, vmem_limit_bytes=60 * 1024 * 1024
        ),
    )(block, gate_up, bias_all, down, down_bias, hidden_state)


def dense_body(
    attn_out,
    out_weight,
    out_bias,
    residual_in,
    norm_gain,
    router_weight,
    router_bias,
    expert_ids,
    filled_rows,
    gate_up,
    gate_up_bias,
    down_weight,
    down_bias,
    next_gain,
):
    tok_rows = residual_in.shape[0]
    experts_all = gate_up.shape[0] * lax.axis_size("expert")
    summed = project(attn_out, out_weight)
    hidden_state = residual_in.astype(jnp.float32) + summed + out_bias
    normed_in = normalize(hidden_state, norm_gain).astype(jnp.bfloat16)
    logits = jnp.dot(normed_in, router_weight, preferred_element_type=jnp.float32) + router_bias
    hits = expert_ids[:, :, None] == jnp.arange(experts_all, dtype=jnp.int32)
    chosen = jnp.sum(jnp.where(hits, logits[:, None, :], 0.0), axis=-1)
    route_probs = jax.nn.softmax(chosen, axis=-1)
    live_rows = jnp.arange(tok_rows, dtype=jnp.int32) < filled_rows[0]
    route_weights = route_probs * live_rows[:, None].astype(jnp.float32)
    spread = jnp.sum(jnp.where(hits, route_weights[:, :, None], 0.0), axis=1)
    coarse = lax.reduce_precision(spread, 8, 7)
    spare = 64 - 2 * experts_all
    block = jnp.concatenate(
        [
            normed_in,
            coarse.astype(jnp.bfloat16),
            (spread - coarse).astype(jnp.bfloat16),
            jnp.zeros((tok_rows, spare), jnp.bfloat16),
        ],
        axis=1,
    )
    stream_full = experts(
        block, gate_up[0], gate_up_bias[0], down_weight[0], down_bias, hidden_state
    )
    return (
        stream_full.astype(jnp.bfloat16),
        normalize(stream_full, next_gain).astype(jnp.bfloat16),
    )


def body(*arrays):
    residual_in, gate_up, down_weight = arrays[3], arrays[9], arrays[11]
    dp_size, expert_size = lax.axis_size("dp"), lax.axis_size("expert")
    token_rows = residual_in.shape[0] * dp_size * expert_size
    weight_rows = dp_size * (2 * gate_up.shape[2] + down_weight.shape[1])
    if gate_up.shape[0] == 1 and expert_size == 8 and dp_size == 4 and 2 * token_rows <= weight_rows:
        return dense_body(*arrays)
    return routed_body(*arrays)


def solution(mesh):
    return jax.shard_map(
        body,
        mesh=mesh,
        in_specs=(
            P("dp", "expert"),
            P("expert", None),
            P(),
            P(("dp", "expert"), None),
            P(),
            P(),
            P(),
            P(("dp", "expert"), None),
            P(("dp", "expert")),
            P("expert", None, "dp", None),
            P("expert", None, None),
            P("expert", "dp", None),
            P("expert", None),
            P(),
        ),
        out_specs=(P(("dp", "expert"), None), P(("dp", "expert"), None)),
        check_vma=False,
    )
```

```python
import functools

import jax
import jax.numpy as jnp
from jax import lax
from jax.experimental import pallas as pl
from jax.experimental.pallas import tpu as pltpu
from jax.sharding import PartitionSpec as P

EPS = 1e-05
LIMIT = 7.0
ALPHA = 1.702


def normalize(values, gain):
    return values * lax.rsqrt(jnp.mean(values * values, axis=-1, keepdims=True) + EPS) * gain


def activate(gate_part, up_part):
    gate_part = jnp.minimum(gate_part, LIMIT)
    up_part = jnp.clip(up_part, -LIMIT, LIMIT)
    return ((up_part + 1.0) * gate_part * jax.nn.sigmoid(ALPHA * gate_part)).astype(jnp.bfloat16)


def hidden_units(row_block, pair_weights, bias_part):
    numbers = (((1,), (1,)), ((), ()))
    gate_part = (
        lax.dot_general(row_block, pair_weights[0], numbers, preferred_element_type=jnp.float32)
        + bias_part[0]
    )
    up_part = (
        lax.dot_general(row_block, pair_weights[1], numbers, preferred_element_type=jnp.float32)
        + bias_part[1]
    )
    return activate(gate_part, up_part)


def routed_body(
    attn_out,
    out_weight,
    out_bias,
    residual_in,
    norm_gain,
    router_weight,
    router_bias,
    expert_ids,
    filled_rows,
    gate_up,
    gate_up_bias,
    down_weight,
    down_bias,
    next_gain,
):
    local_count = gate_up.shape[0]
    model_width = residual_in.shape[1]
    tok_rows = residual_in.shape[0]
    top_count = expert_ids.shape[1]
    experts_all = local_count * lax.axis_size("expert")
    capacity = 2 * tok_rows * top_count // experts_all
    row_block = attn_out
    summed = lax.psum_scatter(
        jnp.dot(row_block, out_weight, preferred_element_type=jnp.float32).astype(jnp.bfloat16),
        "expert",
        scatter_dimension=0,
        tiled=True,
    ).astype(jnp.float32)
    hidden_state = residual_in.astype(jnp.float32) + summed + out_bias
    normed_in = normalize(hidden_state, norm_gain).astype(jnp.bfloat16)
    logits = jnp.dot(normed_in, router_weight, preferred_element_type=jnp.float32) + router_bias
    chosen = jnp.take_along_axis(logits, expert_ids, axis=1)
    route_probs = jax.nn.softmax(chosen, axis=-1)
    live_rows = jnp.arange(tok_rows, dtype=jnp.int32) < filled_rows[0]
    route_weights = route_probs * live_rows[:, None].astype(jnp.float32)
    flat_ids = expert_ids.reshape(-1)
    onehot = (flat_ids[:, None] == jnp.arange(experts_all, dtype=jnp.int32)[None, :]).astype(
        jnp.int32
    )
    before = jnp.cumsum(onehot, axis=0) - onehot
    slot_ids = flat_ids * capacity + jnp.sum(before * onehot, axis=1)
    placing = (
        jnp.arange(experts_all * capacity, dtype=jnp.int32)[:, None] == slot_ids[None, :]
    ).astype(jnp.bfloat16)
    repeated = jnp.repeat(normed_in, top_count, axis=0)
    outgoing = jnp.dot(placing, repeated, preferred_element_type=jnp.float32).astype(jnp.bfloat16)
    outgoing = outgoing.reshape(experts_all, capacity, model_width)
    arrived = lax.all_to_all(outgoing, "expert", split_axis=0, concat_axis=0, tiled=True)
    arrived = arrived.reshape(-1, local_count, capacity, model_width)
    row_block = arrived[:, 0].reshape(-1, model_width)
    bias_pair = gate_up_bias[0]
    hidden = hidden_units(
        row_block, lax.all_gather(gate_up[0], "dp", axis=1, tiled=True), bias_pair
    )
    summed_rows = jnp.dot(
        hidden,
        lax.all_gather(down_weight[0], "dp", axis=0, tiled=True),
        preferred_element_type=jnp.float32,
    )
    results = [(summed_rows + down_bias[0]).astype(jnp.bfloat16).reshape(-1, capacity, model_width)]
    answered = jnp.stack(results, axis=1).reshape(-1, capacity, model_width)
    returned = lax.all_to_all(answered, "expert", split_axis=0, concat_axis=0, tiled=True)
    returned = returned.reshape(experts_all * capacity, model_width)
    picked = returned[slot_ids].astype(jnp.float32).reshape(tok_rows, top_count, model_width)
    mixture = jnp.sum(picked * route_weights[:, :, None], axis=1)
    stream_full = hidden_state + mixture
    return (
        stream_full.astype(jnp.bfloat16),
        normalize(stream_full, next_gain).astype(jnp.bfloat16),
    )


def place():
    z, e = lax.axis_index("dp"), lax.axis_index("expert")
    y, x, core = e // 4, (e // 2) % 2, e % 2
    at = lambda yy, xx, cc: yy * 4 + xx * 2 + cc
    return dict(
        z=z, e=e, y=y, x=x, core=core,
        s=at(y, x, 1 - core), xn=at(y, 1 - x, core), yn=at(1 - y, x, core),
        dn=at(1 - y, 1 - x, core),
    )


def remote(src, dst, send_sem, recv_sem, device):
    return pltpu.make_async_remote_copy(
        src_ref=src, dst_ref=dst, send_sem=send_sem, recv_sem=recv_sem,
        device_id=device, device_id_type=pl.DeviceIdType.MESH,
    )


def greet(devices):
    barrier = pltpu.get_barrier_semaphore()
    for device in devices:
        pl.semaphore_signal(
            barrier, inc=1, device_id=device, device_id_type=pl.DeviceIdType.MESH
        )
    pl.semaphore_wait(barrier, len(devices))


class PlaneSum:
    def __init__(self, here, parts, paired, from_x, from_y, last, send, recv, sent):
        self.here, self.parts, self.paired = here, parts, paired
        self.from_x, self.from_y, self.last = from_x, from_y, last
        self.send, self.recv, self.sent = send, recv, sent
        self.half = parts.shape[4] // 2

    def put(self, src, dst, k, lane, to):
        copy = remote(
            src, dst, self.send.at[k, lane], self.recv.at[k, lane], (self.here["z"], self.here[to])
        )
        copy.start()
        self.sent.append(copy)

    def take(self, dst, k, lane, to):
        remote(
            dst, dst, self.send.at[k, lane], self.recv.at[k, lane], (self.here["z"], self.here[to])
        ).wait_recv()

    def pair(self, k):
        self.put(self.parts.at[k, 1 - self.here["core"]], self.paired.at[k], k, 0, "s")

    def first(self, k):
        core, x, y, half = self.here["core"], self.here["x"], self.here["y"], self.half
        self.take(self.paired.at[k], k, 0, "s")

        @pl.loop(0, 4)
        def _(i):
            yy, xx = i // 2, i % 2
            self.parts[k, core, yy, xx] = (
                self.parts[k, core, yy, xx].astype(jnp.float32)
                + self.paired[k, yy, xx].astype(jnp.float32)
            ).astype(jnp.bfloat16)

        low, high = pl.ds(0, half), pl.ds(half, half)
        self.put(self.parts.at[k, core, :, 1 - x, low], self.from_x.at[k], k, 1, "xn")
        self.put(self.parts.at[k, core, 1 - y, :, high], self.from_y.at[k], k, 2, "yn")

    def second(self, k):
        core, x, y, half = self.here["core"], self.here["x"], self.here["y"], self.half
        low, high = pl.ds(0, half), pl.ds(half, half)

        def add(yy, xx, rows, more):
            self.parts[k, core, yy, xx, rows] = (
                self.parts[k, core, yy, xx, rows].astype(jnp.float32) + more.astype(jnp.float32)
            ).astype(jnp.bfloat16)

        self.take(self.from_x.at[k], k, 1, "xn")
        add(1 - y, x, low, self.from_x[k, 1 - y])
        self.put(self.parts.at[k, core, 1 - y, x, low], self.last.at[k, low], k, 3, "yn")
        self.take(self.from_y.at[k], k, 2, "yn")
        add(y, 1 - x, high, self.from_y[k, 1 - x])
        self.put(self.parts.at[k, core, y, 1 - x, high], self.last.at[k, high], k, 4, "xn")

    def third(self, k):
        core, x, y, half = self.here["core"], self.here["x"], self.here["y"], self.half
        low, high = pl.ds(0, half), pl.ds(half, half)
        self.take(self.last.at[k, low], k, 3, "yn")
        self.take(self.last.at[k, high], k, 4, "xn")
        own = self.parts[k, core, y, x].astype(jnp.float32) + self.last[k].astype(jnp.float32)
        more = jnp.concatenate([self.from_x[k, y], self.from_y[k, x]], axis=0)
        return own + more.astype(jnp.float32)


def plane_scratch(groups, rows, width):
    return [
        pltpu.VMEM((groups, 2, 2, 2, rows, width), jnp.bfloat16),
        pltpu.VMEM((groups, 2, 2, rows, width), jnp.bfloat16),
        pltpu.VMEM((groups, 2, rows // 2, width), jnp.bfloat16),
        pltpu.VMEM((groups, 2, rows // 2, width), jnp.bfloat16),
        pltpu.VMEM((groups, rows, width), jnp.bfloat16),
        pltpu.SemaphoreType.DMA((groups, 5)),
        pltpu.SemaphoreType.DMA((groups, 5)),
    ]


CHUNKS = 2


def projection_kernel(
    attn, weight, out, held, lsem, parts, paired, from_x, from_y, last, send, recv
):
    here = place()
    rows = attn.shape[2] // CHUNKS
    load = pltpu.make_async_copy(weight, held, lsem)
    load.start()
    greet([(here["z"], here[name]) for name in ("s", "xn", "yn")])
    sent = []
    plane = PlaneSum(here, parts, paired, from_x, from_y, last, send, recv, sent)
    load.wait()

    def multiply(chunk, core):
        block = attn[:, core, chunk * rows : (chunk + 1) * rows].reshape(4 * rows, attn.shape[3])
        result = lax.dot_general(
            block, held[...], (((1,), (1,)), ((), ())), preferred_element_type=jnp.float32
        ).astype(jnp.bfloat16)
        for i in range(4):
            parts[chunk, core, i // 2, i % 2] = result[i * rows : (i + 1) * rows]

    for chunk in range(CHUNKS):
        multiply(chunk, 1 - here["core"])
        plane.pair(chunk)
    for chunk in range(CHUNKS):
        multiply(chunk, here["core"])
        plane.first(chunk)
    for chunk in range(CHUNKS):
        plane.second(chunk)
    for chunk in range(CHUNKS):
        out[chunk * rows : (chunk + 1) * rows] = plane.third(chunk)
    for copy in sent:
        copy.wait_send()


def project(attn_out, out_weight):
    tokens, features = attn_out.shape
    width = out_weight.shape[1]
    rows = tokens // 8
    vmem = pl.BlockSpec(memory_space=pltpu.VMEM)
    return pl.pallas_call(
        projection_kernel,
        out_shape=jax.ShapeDtypeStruct((rows, width), jnp.float32),
        in_specs=[vmem, pl.BlockSpec(memory_space=pl.ANY)],
        out_specs=vmem,
        scratch_shapes=[pltpu.VMEM((width, features), jnp.bfloat16), pltpu.SemaphoreType.DMA]
        + plane_scratch(CHUNKS, rows // CHUNKS, width),
        compiler_params=pltpu.CompilerParams(
            collective_id=0, has_side_effects=True, vmem_limit_bytes=60 * 1024 * 1024
        ),
    )(attn_out.reshape(4, 2, rows, features), out_weight.T)


def experts_kernel(
    groups, block, gate_up, bias_all, down, down_bias, hidden_state, full_out,
    tok, bias_pair, gu, dw, acc, zin, zout, gsend, grecv, zsend, zrecv, lsem,
    parts, paired, from_x, from_y, last, send, recv,
):
    here = place()
    z, e, core = here["z"], here["e"], here["core"]
    rows, width = hidden_state.shape
    half = rows // 2
    low, high = pl.ds(0, half), pl.ds(half, half)
    loads = [
        pltpu.make_async_copy(block, tok.at[z, e], lsem.at[0]),
        pltpu.make_async_copy(gate_up, gu, lsem.at[1]),
        pltpu.make_async_copy(down, dw, lsem.at[2]),
    ]
    for load in loads:
        load.start()
    units = bias_pair.shape[1]
    bias_pair[...] = sum(
        jnp.where(z == j, bias_all[:, j * units : (j + 1) * units], 0.0) for j in range(groups)
    )
    group = [z] + [z + j - 2 * sum(b * ((z // b) % 2) for b in (1, 2, 4) if j & b) for j in range(1, groups)]
    ring = [(group[j], e) for j in range(1, groups)]
    greet([(z, here[name]) for name in ("s", "xn", "yn")] + ring)
    sent = []
    plane = PlaneSum(here, parts, paired, from_x, from_y, last, send, recv, sent)

    def put(src, dst, k, lane, device):
        copy = remote(src, dst, gsend.at[k, lane], grecv.at[k, lane], device)
        copy.start()
        sent.append(copy)

    def take(dst, k, lane, device):
        remote(dst, dst, gsend.at[k, lane], grecv.at[k, lane], device).wait_recv()

    sib, to_x, to_y = (z, here["s"]), (z, here["xn"]), (z, here["yn"])

    def enter(k):
        g = group[k]
        if k > 0:
            take(tok.at[g, e], k, 0, ring[k - 1])
        src = block if k == 0 else tok.at[g, e]
        put(src, tok.at[g, e], k, 1, to_x)
        put(src, tok.at[g, e], k, 2, to_y)
        for j in ((1, 2), (3,))[k] if k < 2 else ():
            put(block, tok.at[z, e], j, 0, ring[j - 1])
        put(src, tok.at[g, e], k, 5, sib)

    def across(k):
        g, xn, yn = group[k], here["xn"], here["yn"]
        take(tok.at[g, xn], k, 1, to_x)
        if k % 2 == 0:
            put(tok.at[g, xn, low], tok.at[g, xn, low], k, 3, to_y)
        put(tok.at[g, xn], tok.at[g, xn], k, 6, sib)
        take(tok.at[g, yn], k, 2, to_y)
        if k % 2 == 0:
            put(tok.at[g, yn, high], tok.at[g, yn, high], k, 4, to_x)
        put(tok.at[g, yn], tok.at[g, yn], k, 7, sib)

    def corner(k):
        g, dn = group[k], here["dn"]
        if k % 2 == 0:
            take(tok.at[g, dn, low], k, 3, to_y)
            take(tok.at[g, dn, high], k, 4, to_x)
            put(tok.at[g, dn], tok.at[g, dn], k + 1, 3, ring[0])
        else:
            take(tok.at[g, dn], k, 3, ring[0])
        put(tok.at[g, dn], tok.at[g, dn], k, 8, sib)

    def compute(k):
        g = group[k]
        for lane, name in ((5, "e"), (6, "xn"), (7, "yn"), (8, "dn")):
            other = here[name] + 1 - 2 * core
            take(tok.at[g, other], k, lane, sib)
        if k == 0:
            for load in loads:
                load.wait()

        @pl.loop(0, 2)
        def _(m):
            mine = pl.ds(m * 4, 4)
            values = tok[g, mine, :, :width].reshape(4 * rows, width)
            hidden = hidden_units(values, (gu[0], gu[1]), (bias_pair[0:1], bias_pair[1:2]))
            part = jnp.dot(hidden, dw[...], preferred_element_type=jnp.float32)
            part = part + jnp.where(z == 0, down_bias[...], 0.0)
            tail = tok[g, mine, :, tok.shape[3] - 128 :].reshape(4 * rows, 128)
            lane = lax.broadcasted_iota(jnp.int32, tail.shape, 1) - 64
            picked = (lane == e) | (lane == e + 8)
            share = jnp.sum(
                jnp.where(picked, tail.astype(jnp.float32), 0.0), axis=1, keepdims=True
            )
            part = (part * share).astype(jnp.bfloat16)
            for i in range(4):
                parts[k, i % 2, m, i // 2] = part[i * rows : (i + 1) * rows]

        plane.pair(k)

    def leave(k):
        total = plane.third(k)
        if k == 0:
            acc[...] = total
            return
        zout[k - 1] = total.astype(jnp.bfloat16)
        copy = remote(
            zout.at[k - 1], zin.at[k - 1], zsend.at[k - 1], zrecv.at[k - 1], (group[k], e)
        )
        copy.start()
        sent.append(copy)

    for step in range(groups + 8):
        for delay, stage in (
            (0, enter), (1, across), (2, corner), (6, leave),
            (5, plane.second), (4, plane.first), (3, compute),
        ):
            if 0 <= step - delay < groups:
                stage(step - delay)
    full = hidden_state[...] + acc[...]
    for k in range(groups - 1):
        remote(zin.at[k], zin.at[k], zsend.at[k], zrecv.at[k], (group[k + 1], e)).wait_recv()
        full = full + zin[k].astype(jnp.float32)
    full_out[...] = full
    for copy in sent:
        copy.wait_send()


def experts(block, gate_up, bias_all, down, down_bias, hidden_state):
    groups = lax.axis_size("dp")
    rows, width = hidden_state.shape
    wide = block.shape[1]
    vmem = pl.BlockSpec(memory_space=pltpu.VMEM)
    anywhere = pl.BlockSpec(memory_space=pl.ANY)
    return pl.pallas_call(
        functools.partial(experts_kernel, groups),
        out_shape=jax.ShapeDtypeStruct((rows, width), jnp.float32),
        in_specs=[vmem, anywhere, vmem, anywhere, vmem, vmem],
        out_specs=vmem,
        scratch_shapes=[
            pltpu.VMEM((groups, 8, rows, wide), jnp.bfloat16),
            pltpu.VMEM(gate_up.shape[:2], jnp.float32),
            pltpu.VMEM(gate_up.shape, jnp.bfloat16),
            pltpu.VMEM(down.shape, jnp.bfloat16),
            pltpu.VMEM((rows, width), jnp.float32),
            pltpu.VMEM((groups - 1, rows, width), jnp.bfloat16),
            pltpu.VMEM((groups - 1, rows, width), jnp.bfloat16),
            pltpu.SemaphoreType.DMA((groups, 9)),
            pltpu.SemaphoreType.DMA((groups, 9)),
            pltpu.SemaphoreType.DMA((groups - 1,)),
            pltpu.SemaphoreType.DMA((groups - 1,)),
            pltpu.SemaphoreType.DMA((3,)),
        ]
        + plane_scratch(groups, rows, width),
        compiler_params=pltpu.CompilerParams(
            collective_id=1, has_side_effects=True, vmem_limit_bytes=60 * 1024 * 1024
        ),
    )(block, gate_up, bias_all, down, down_bias, hidden_state)


def dense_body(
    attn_out,
    out_weight,
    out_bias,
    residual_in,
    norm_gain,
    router_weight,
    router_bias,
    expert_ids,
    filled_rows,
    gate_up,
    gate_up_bias,
    down_weight,
    down_bias,
    next_gain,
):
    tok_rows = residual_in.shape[0]
    experts_all = gate_up.shape[0] * lax.axis_size("expert")
    summed = project(attn_out, out_weight)
    hidden_state = residual_in.astype(jnp.float32) + summed + out_bias
    normed_in = normalize(hidden_state, norm_gain).astype(jnp.bfloat16)
    logits = jnp.dot(normed_in, router_weight, preferred_element_type=jnp.float32) + router_bias
    hits = expert_ids[:, :, None] == jnp.arange(experts_all, dtype=jnp.int32)
    chosen = jnp.sum(jnp.where(hits, logits[:, None, :], 0.0), axis=-1)
    route_probs = jax.nn.softmax(chosen, axis=-1)
    live_rows = jnp.arange(tok_rows, dtype=jnp.int32) < filled_rows[0]
    route_weights = route_probs * live_rows[:, None].astype(jnp.float32)
    spread = jnp.sum(jnp.where(hits, route_weights[:, :, None], 0.0), axis=1)
    coarse = lax.reduce_precision(spread, 8, 7)
    spare = 64 - 2 * experts_all
    block = jnp.concatenate(
        [
            normed_in,
            coarse.astype(jnp.bfloat16),
            (spread - coarse).astype(jnp.bfloat16),
            jnp.zeros((tok_rows, spare), jnp.bfloat16),
        ],
        axis=1,
    )
    stream_full = experts(
        block, gate_up[0], gate_up_bias[0], down_weight[0], down_bias, hidden_state
    )
    return (
        stream_full.astype(jnp.bfloat16),
        normalize(stream_full, next_gain).astype(jnp.bfloat16),
    )


def body(*arrays):
    residual_in, gate_up, down_weight = arrays[3], arrays[9], arrays[11]
    dp_size, expert_size = lax.axis_size("dp"), lax.axis_size("expert")
    token_rows = residual_in.shape[0] * dp_size * expert_size
    weight_rows = dp_size * (2 * gate_up.shape[2] + down_weight.shape[1])
    if gate_up.shape[0] == 1 and expert_size == 8 and dp_size == 4 and 2 * token_rows <= weight_rows:
        return dense_body(*arrays)
    return routed_body(*arrays)


def solution(mesh):
    return jax.shard_map(
        body,
        mesh=mesh,
        in_specs=(
            P("dp", "expert"),
            P("expert", None),
            P(),
            P(("dp", "expert"), None),
            P(),
            P(),
            P(),
            P(("dp", "expert"), None),
            P(("dp", "expert")),
            P("expert", None, "dp", None),
            P("expert", None, None),
            P("expert", "dp", None),
            P("expert", None),
            P(),
        ),
        out_specs=(P(("dp", "expert"), None), P(("dp", "expert"), None)),
        check_vma=False,
    )
```
